256 devices in a mesh: freq: 4 (over z_lo), sub: 64 (over x, y, z_hi, core).
Axes of the slice: x: 4, y: 4, z: 8 (z_hi: 2, z_lo: 4; z = z_hi * 4 + z_lo), core: 2. Of those that a mesh axis runs over, the one named last changes fastest.
Arguments:
- sources: float32 [8, 4, 512, 64, 256], P('freq', None, 'sub'), may hold values from -5 to 5
- slowness: float32 [512, 64, 256], P('sub'), may hold values from 0.6 to 1.6
- freq_index: int32 [8], P('freq'), may hold values from 0 to 15
- coverage: int32 [4, 64, 64], P('freq'), may hold values from 0 to 511, as said below
Outputs:
- precond_gradient: float32 [512, 64, 256], P('sub', 'freq')
- delivered: float32 [4, 64, 64, 16, 256], P('freq', 'sub')
The draws below stay inside these ranges and needn't reach their ends.
Inputs may be any that keep to these rules, and one draw needn't show every extreme that they name: `coverage`: each list names 64 distinct tiles of its depth band; a list names exactly 2 tiles of each owner it names and none of the others, so at most 2 of any one owner.
All inputs are finite; a program needn't handle non-finite values.
Results may differ from the reference program's by a relative error of at most 0.00002.
Values sent between devices are 32-bit elements; how exact they have to be, the bound alone decides.
A program may use at most 128 MiB of HBM per device.

```python
import math
import jax
import jax.numpy as jnp
from jax import lax

CX = 8
NZ = 64
NY = 256
PASSES = 4
TPD = 8
CAP = 2
FREQS = 8
NX = 512
TROWS = 16
KF = 64
N_FREQ = 4
N_SUB = 64


def draw_sources(key, part):
    shape = (FREQS, 4, NX, NZ, NY)
    return jnp.clip(jax.random.normal(key, shape, jnp.float32), -5.0, 5.0)


def draw_coverage(key, part):
    total_lists = N_FREQ * N_SUB
    picked = N_SUB // 2
    list_keys = jax.random.split(jax.random.fold_in(key, 11), total_lists)

    def one_list(list_key, list_id):
        owner_key, tile_key, shuffle_key = jax.random.split(list_key, 3)
        owners_all = jnp.arange(N_SUB, dtype=jnp.int32)
        owner_score = jax.random.randint(owner_key, (N_SUB,), 0, 1 << 20) * N_SUB + owners_all
        forced = (list_id == 0) & ((owners_all == 0) | (owners_all == N_SUB - 1))
        owner_score = jnp.where(forced, -1 - owners_all, owner_score)
        owners = jnp.argsort(owner_score, stable=True)[:picked].astype(jnp.int32)
        tiles_all = jnp.arange(TPD, dtype=jnp.int32)
        tile_score = jax.random.randint(tile_key, (picked, TPD), 0, 1 << 20) * TPD + tiles_all[None, :]
        first_low = (owners[:, None] == 0) & (tiles_all[None, :] == 0)
        last_high = (owners[:, None] == N_SUB - 1) & (tiles_all[None, :] == TPD - 1)
        tile_force = (list_id == 0) & (first_low | last_high)
        tile_score = jnp.where(tile_force, -1, tile_score)
        chosen = jnp.argsort(tile_score, axis=1, stable=True)[:, :CAP].astype(jnp.int32)
        numbers = (owners[:, None] * TPD + chosen).reshape(-1)
        shuffle = jax.random.permutation(shuffle_key, KF)
        return numbers[shuffle]
    lists = jax.vmap(one_list)(list_keys, jnp.arange(total_lists, dtype=jnp.int32))
    return lists.reshape(N_FREQ, N_SUB, KF)


def touch_ends(array, stream_key, low, high):
    shape = array.shape
    place = [jax.random.randint(jax.random.fold_in(stream_key, axis), (), 0, shape[axis]) for axis in range(len(shape))]
    array = array.at[tuple(place)].set(low)
    longest = shape.index(max(shape))
    place[longest] = (place[longest] + 1) % shape[longest]
    return array.at[tuple(place)].set(high)


def steps_of(rng, dims, cuts, smallest, top_value):
    gain, own = 1.0, jax.random.fold_in(rng, 6)
    for dim, shards_of in cuts:
        draws = jnp.exp(jax.random.uniform(jax.random.fold_in(own, dim), (shards_of,), jnp.float32, smallest / len(cuts), top_value / len(cuts)))
        gain = gain * jnp.repeat(draws, dims[dim] // shards_of).reshape([-1 if axis == dim else 1 for axis in range(len(dims))])
    return gain


def setup_inputs(seed: int = 0) -> dict:
    streams_of = jax.random.split(jax.random.key(seed), 5)
    sources = draw_sources(jax.random.fold_in(streams_of[4], 71), 0)
    slowness = jnp.clip(jnp.exp(math.log(1.6) - 0.98082923 * jax.random.uniform(streams_of[1], (NX, NZ, NY), jnp.float32) ** steps_of(streams_of[1], (NX, NZ, NY), ((0, 64),), -0.2, 0.2)), 0.6, 1.6)
    freq_index = touch_ends(jax.random.randint(streams_of[2], (FREQS,), 0, 16), jax.random.fold_in(streams_of[2], 1), 0, 15).astype(jnp.int32)
    coverage = draw_coverage(jax.random.fold_in(streams_of[4], 71), 0)
    return {"sources": sources, "slowness": slowness, "freq_index": freq_index, "coverage": coverage}


def smooth_axis(values, axis):
    widths = [(0, 0)] * values.ndim
    widths[axis] = (1, 1)
    padded = jnp.pad(values, widths)
    length = values.shape[axis]
    before = lax.slice_in_dim(padded, 0, length, axis=axis)
    middle = lax.slice_in_dim(padded, 1, length + 1, axis=axis)
    after = lax.slice_in_dim(padded, 2, length + 2, axis=axis)
    return 0.25 * before + 0.5 * middle + 0.25 * after

def smooth_all(values):
    first = smooth_axis(values, values.ndim - 3)
    second = smooth_axis(first, values.ndim - 2)
    return smooth_axis(second, values.ndim - 1)

def one_frequency(forcing, weight, slowness):
    sigma_cells = 0.12 * weight * slowness
    diag_real = 0.875 - sigma_cells
    diag_imag = sigma_cells
    diag_norm = diag_real * diag_real + diag_imag * diag_imag
    force_real = forcing[0::2]
    force_imag = forcing[1::2]
    real_part = jnp.zeros(force_real.shape, jnp.float32)
    imag_part = jnp.zeros(force_real.shape, jnp.float32)
    for step in range(PASSES):
        applied_real = real_part - sigma_cells * (real_part + imag_part) - smooth_all(real_part)
        applied_imag = imag_part - sigma_cells * (imag_part - real_part) - smooth_all(imag_part)
        resid_real = force_real - applied_real
        resid_imag = force_imag - applied_imag
        real_part = real_part + (resid_real * diag_real + resid_imag * diag_imag) / diag_norm
        imag_part = imag_part + (resid_imag * diag_real - resid_real * diag_imag) / diag_norm
    grad_term = weight * (real_part[0] * real_part[1] - imag_part[0] * imag_part[1])
    illum_term = weight * (real_part[0] * real_part[0] + imag_part[0] * imag_part[0])
    return (grad_term, illum_term)

def reference(sources, slowness, freq_index, coverage):
    weights = 1.0 + freq_index.astype(jnp.float32) / 16.0
    terms = lax.map(lambda pair: one_frequency(pair[0], pair[1], slowness), (sources, weights))
    gradient = lax.optimization_barrier(jnp.sum(terms[0], axis=0))
    illum = lax.optimization_barrier(jnp.sum(terms[1], axis=0))
    precond = gradient / jnp.sqrt(illum + 1.0)
    depth = NZ // N_FREQ
    tiles = precond.reshape(N_SUB, CX, N_FREQ, depth, NY).transpose(2, 0, 1, 3, 4)
    tiles = tiles.reshape(N_FREQ, N_SUB * TPD, TROWS, NY)
    group_ids = jnp.arange(N_FREQ, dtype=jnp.int32)[:, None, None]
    delivered = tiles[group_ids, coverage]
    return (precond, delivered)
```

```python
import jax
import jax.numpy as jnp
from jax import lax
from jax.experimental import pallas as pl
from jax.experimental.pallas import tpu as pltpu
from jax.sharding import PartitionSpec as P

MESH = pl.DeviceIdType.MESH
CX = 8
BAND = 16
ROUNDS = ((3, 8), (2, 3), (1, 2), (0, 1))


def smooth_plane(t):
    rows, cols = t.shape
    row = lax.broadcasted_iota(jnp.int32, t.shape, 0)
    col = lax.broadcasted_iota(jnp.int32, t.shape, 1)
    before = jnp.where(row == 0, 0.0, pltpu.roll(t, 1, 0))
    after = jnp.where(row == rows - 1, 0.0, pltpu.roll(t, rows - 1, 0))
    t = before + after + (t + t)
    before = jnp.where(col == 0, 0.0, pltpu.roll(t, 1, 1))
    after = jnp.where(col == cols - 1, 0.0, pltpu.roll(t, cols - 1, 1))
    return before + after + (t + t)


def kernel(
    src_hbm, slow_hbm, freq_ref, cover_ref, pre_ref, deliv_ref,
    src, slow, coef, v, halo, slow_x, coef_x, corr, gi, rsr, ag,
    load_sem, slow_sem, halo_ssem, halo_rsem, sx_ssem, sx_rsem, core_ssem, core_rsem,
    rs_ssem, rs_rsem, z_ssem, z_rsem, p1_ssem, p1_rsem, p2_ssem, p2_rsem, cc_ssem, cc_rsem,
):
    f = lax.axis_index("freq")
    s = lax.axis_index("sub")
    c = lax.rem(s, 2)
    zh = lax.rem(s // 2, 2)
    y = lax.rem(s // 4, 4)
    x = s // 16

    def dev(x_, y_, z_, c_):
        return {"freq": f, "sub": ((x_ * 4 + y_) * 2 + z_) * 2 + c_}

    def layer(m):
        return m + c * (CX - 1 - 2 * m)

    x_dev = {"freq": f, "sub": lax.rem(s + 2 * c + 63, 64)}
    c_dev = dev(x, y, zh, 1 - c)
    z_dev = dev(x, y, 1 - zh, c)
    xs = [dev(lax.rem(x + k, 4), y, zh, c) for k in (1, 2, 3)]
    ys = [dev(x, lax.rem(y + k, 4), zh, c) for k in (1, 2, 3)]
    fs = [{"freq": lax.rem(f + k, 4), "sub": s} for k in (1, 2, 3)]
    has_x = jnp.where((s == 0) | (s == 63), 0.0, 1.0).astype(jnp.float32)
    quarter_x = has_x * (0.25 / 16.0)

    slow_loads = [
        pltpu.make_async_copy(slow_hbm.at[layer(m)], slow.at[m], slow_sem.at[m]) for m in range(CX)
    ]
    loads = [
        pltpu.make_async_copy(src_hbm.at[:, :, layer(m)], src.at[m], load_sem.at[m]) for m in range(CX)
    ]
    for m in (0, 1, 2, 7, 3, 4, 5, 6):
        slow_loads[m].start()
        loads[m].start()

    barrier = pltpu.get_barrier_semaphore()
    partners = [x_dev, c_dev, z_dev] + xs + ys + fs
    for who in partners:
        pl.semaphore_signal(barrier, inc=1, device_id=who, device_id_type=MESH)

    weights = [1.0 + freq_ref[g].astype(jnp.float32) / 16.0 for g in range(2)]

    def remote(src_ref, dst_ref, ssem, rsem, who):
        return pltpu.make_async_remote_copy(
            src_ref=src_ref, dst_ref=dst_ref, send_sem=ssem, recv_sem=rsem,
            device_id=who, device_id_type=MESH,
        )

    def coefs(sigma):
        real = 0.875 - sigma
        inv = 1.0 / (real * real + sigma * sigma)
        return real * inv, sigma * inv

    def over_fields(step):
        def one(i, carry):
            step(i // 2, lax.rem(i, 2) * 2)
            return carry
        lax.fori_loop(0, 4, one, 0)

    def put(ref, where, g, q, h, cr, ci, add=False):
        real = h[0] * cr + h[1] * ci
        imag = h[1] * cr - h[0] * ci
        if add:
            real = real + ref[where + (g, q)]
            imag = imag + ref[where + (g, q + 1)]
        ref[where + (g, q)] = real
        ref[where + (g, q + 1)] = imag

    def first(m):
        for g in range(2):
            cr, ci = coefs((0.12 * weights[g]) * slow[m])
            coef[m, g, 0] = cr
            coef[m, g, 1] = ci
            for q in (0, 2):
                put(v, (0, m + 1), g, q, (src[m, g, q], src[m, g, q + 1]), cr, ci)

    def relax(level, m):
        def step(g, q):
            h = []
            for part in (0, 1):
                mid = v[level, m + 1, g, q + part]
                t = v[level, m, g, q + part] + v[level, m + 2, g, q + part] + (mid + mid)
                h.append(src[m, g, q + part] + (smooth_plane(t) * (1.0 / 64.0) - 0.125 * mid))
            put(v, (level + 1, m + 1), g, q, h, coef[m, g, 0], coef[m, g, 1])
        over_fields(step)

    def relax_range(level, lo, hi):
        def one(m, carry):
            relax(level, m)
            return carry
        lax.fori_loop(lo, hi, one, 0)

    def first_range(lo, hi):
        def one(m, carry):
            first(m)
            return carry
        lax.fori_loop(lo, hi, one, 0)

    for level in range(3):
        def clear(i, carry):
            v[level, 0, i // 4, lax.rem(i, 4)] = jnp.zeros((64, 256), jnp.float32)
            return carry
        lax.fori_loop(0, 8, clear, 0)

    x_sends = [
        remote(v.at[n, 1], halo.at[n], halo_ssem.at[n], halo_rsem.at[n], x_dev) for n in range(3)
    ]
    slow_send = remote(slow.at[0], slow_x, sx_ssem, sx_rsem, x_dev)
    c_sends = [
        remote(v.at[n, 8], v.at[n, 9], core_ssem.at[n], core_rsem.at[n], c_dev) for n in range(3)
    ]

    for m in (0, 1, 2):
        slow_loads[m].wait()
        loads[m].wait()
        if m == 0:
            first(0)
            pl.semaphore_wait(barrier, len(partners))
            x_sends[0].start()
            slow_send.start()
        elif m == 1:
            first(1)
            relax(0, 0)
            x_sends[1].start()
        else:
            first(2)
            relax(0, 1)
            relax(1, 0)
            x_sends[2].start()

    for m in (7, 3, 4, 5, 6):
        slow_loads[m].wait()
        loads[m].wait()
        if m == 7:
            first_range(7, 8)
            c_sends[0].start()
    first_range(3, 7)
    for level in range(3):
        c_sends[level].wait_recv()
        relax_range(level, 7, 8)
        if level < 2:
            c_sends[level + 1].start()
        relax_range(level, 2 - level, 7)

    def finish(lo, hi):
        def one(m, carry):
            for b in range(4):
                rows = pl.ds(b * BAND, BAND)
                grad = None
                for g in range(2):
                    ur, ui, ar, ai = [v[3, m + 1, g, q, rows, :] for q in range(4)]
                    gg = weights[g] * (ur * ar - ui * ai)
                    ii = weights[g] * (ur * ur + ui * ui)
                    grad, illum = (gg, ii) if grad is None else (grad + gg, illum + ii)
                gi[b, m, 0] = grad
                gi[b, m, 1] = illum
            return carry
        lax.fori_loop(lo, hi, one, 0)

    sent = []

    def rs_copies(r):
        lo, hi = ROUNDS[r]
        n = pl.ds(lo, hi - lo)
        return [
            remote(gi.at[lax.rem(f + k + 1, 4), n], rsr.at[k, n],
                   rs_ssem.at[r, k], rs_rsem.at[r, k], fs[k])
            for k in range(3)
        ]

    def block(r, *where):
        lo, hi = ROUNDS[r]
        return ag.at[where + (pl.ds(lo, hi - lo),)]

    def z_copy(r):
        b = block(r, x, y, zh, c)
        return remote(b, b, z_ssem.at[r], z_rsem.at[r], z_dev)

    def p1_copies(r, flow):
        b = block(r, x, y, zh, c) if flow == 0 else block(r, x, y, 1 - zh, c)
        to = xs if flow == 0 else ys
        return [remote(b, b, p1_ssem.at[flow, r, k], p1_rsem.at[flow, r, k], to[k]) for k in range(3)]

    every = slice(None)

    def p2_copies(r, flow):
        b = block(r, every, y, zh, c) if flow == 0 else block(r, x, every, 1 - zh, c)
        to = ys if flow == 0 else xs
        return [remote(b, b, p2_ssem.at[flow, r, k], p2_rsem.at[flow, r, k], to[k]) for k in range(3)]

    def cc_copy(r):
        b = block(r, every, every, every, c)
        return remote(b, b, cc_ssem.at[r], cc_rsem.at[r], c_dev)

    def start(copies):
        for copy in copies:
            copy.start()
            sent.append(copy)

    def arrived(copies):
        for copy in copies:
            copy.wait_recv()

    def reduce_start(r):
        finish(*ROUNDS[r])
        start(rs_copies(r))

    def gather_start(r):
        arrived(rs_copies(r))
        lo, hi = ROUNDS[r]

        def one(m, carry):
            grad = gi[f, m, 0] + rsr[0, m, 0] + rsr[1, m, 0] + rsr[2, m, 0]
            illum = gi[f, m, 1] + rsr[0, m, 1] + rsr[1, m, 1] + rsr[2, m, 1]
            pre = grad / jnp.sqrt(illum + 1.0)
            ag[x, y, zh, c, m] = pre
            pre_ref[layer(m)] = pre
            return carry
        lax.fori_loop(lo, hi, one, 0)
        start([z_copy(r)])
        start(p1_copies(r, 0))

    def gather_middle(r):
        arrived([z_copy(r)])
        start(p1_copies(r, 1))
        arrived(p1_copies(r, 0))
        start(p2_copies(r, 0))
        arrived(p1_copies(r, 1))
        start(p2_copies(r, 1))

    def gather_end(r):
        arrived(p2_copies(r, 0))
        arrived(p2_copies(r, 1))
        start([cc_copy(r)])

    C2, C3A, C3B, D2, D3 = range(5)

    def correct(ref, where, cf, terms, minus=None, add=False):
        def step(g, q):
            h = []
            for part in (0, 1):
                t = None
                for scale, tref, twhere in terms:
                    one = scale * tref[twhere + (g, q + part)]
                    t = one if t is None else t + one
                k = smooth_plane(t)
                if minus is not None:
                    k = k - 0.125 * minus[0][minus[1] + (g, q + part)]
                h.append(k)
            put(ref, where, g, q, h, cf[g, 0], cf[g, 1], add)
        over_fields(step)

    half = 0.5 / 16.0
    quarter = 0.25 / 16.0

    reduce_start(0)
    slow_send.wait_recv()
    for g in range(2):
        cr, ci = coefs((0.12 * weights[g]) * slow_x[...])
        coef_x[g, 0] = cr
        coef_x[g, 1] = ci
    correct(corr, (D2,), coef_x, [(quarter, v, (0, 1))])
    gather_start(0)

    x_sends[0].wait_recv()
    correct(corr, (C2,), coef.at[0], [(quarter_x, halo, (0,))])
    correct(corr, (C3B,), coef.at[1], [(quarter, corr, (C2,))])
    correct(v, (3, 3), coef.at[2], [(quarter, corr, (C3B,))], add=True)
    reduce_start(1)
    gather_middle(0)
    correct(corr, (D3,), coef_x, [(half, corr, (D2,)), (quarter, v, (1, 1)), (quarter, corr, (C2,))],
            minus=(corr, (D2,)))
    gather_start(1)
    gather_end(0)
    gather_middle(1)

    x_sends[1].wait_recv()
    correct(corr, (C3A,), coef.at[0],
            [(half, corr, (C2,)), (quarter_x, halo, (1,)), (quarter_x, corr, (D2,))],
            minus=(corr, (C2,)))
    correct(v, (3, 2), coef.at[1], [(half, corr, (C3B,)), (quarter, corr, (C3A,))],
            minus=(corr, (C3B,)), add=True)
    reduce_start(2)
    correct(v, (3, 1), coef.at[0],
            [(half, corr, (C3A,)), (quarter, corr, (C3B,)), (quarter_x, corr, (D3,))],
            minus=(corr, (C3A,)), add=True)
    gather_end(1)
    gather_start(2)
    gather_middle(2)
    gather_end(2)

    x_sends[2].wait_recv()
    correct(v, (3, 1), coef.at[0], [(quarter_x, halo, (2,))], add=True)
    reduce_start(3)
    gather_start(3)
    gather_middle(3)
    gather_end(3)
    for r in range(4):
        arrived([cc_copy(r)])

    def pick(k, carry):
        tile = cover_ref[0, s, k]
        o = tile // CX
        j = lax.rem(tile, CX)
        oc = lax.rem(o, 2)
        m = j + oc * (CX - 1 - 2 * j)
        deliv_ref[0, 0, k] = ag[o // 16, lax.rem(o // 4, 4), lax.rem(o // 2, 2), oc, m]
        return carry
    lax.fori_loop(0, deliv_ref.shape[2], pick, 0)

    for copy in x_sends + [slow_send] + c_sends + sent:
        copy.wait_send()


def body(sources, slowness, freq_index, coverage):
    groups, parts, cx, nz, ny = sources.shape
    f32 = jnp.float32
    tiles = coverage.shape[2]
    vm = pltpu.VMEM
    dma = pltpu.SemaphoreType.DMA
    field = (groups, parts, nz, ny)
    return pl.pallas_call(
        kernel,
        name="inversion_step",
        out_shape=(
            jax.ShapeDtypeStruct((cx, BAND, ny), f32),
            jax.ShapeDtypeStruct((1, 1, tiles, BAND, ny), f32),
        ),
        in_specs=[
            pl.BlockSpec(memory_space=pl.ANY),
            pl.BlockSpec(memory_space=pl.ANY),
            pl.BlockSpec(memory_space=pltpu.SMEM),
            pl.BlockSpec(memory_space=pltpu.SMEM),
        ],
        out_specs=(pl.BlockSpec(memory_space=pltpu.VMEM), pl.BlockSpec(memory_space=pltpu.VMEM)),
        scratch_shapes=[
            vm((cx,) + field, f32),
            vm((cx, nz, ny), f32),
            vm((cx, groups, 2, nz, ny), f32),
            vm((4, cx + 2) + field, f32),
            vm((3,) + field, f32),
            vm((nz, ny), f32),
            vm((groups, 2, nz, ny), f32),
            vm((5,) + field, f32),
            vm((4, cx, 2, BAND, ny), f32),
            vm((3, cx, 2, BAND, ny), f32),
            vm((4, 4, 2, 2, cx, BAND, ny), f32),
            dma((cx,)), dma((cx,)),
            dma((3,)), dma((3,)), dma, dma, dma((3,)), dma((3,)),
            dma((4, 3)), dma((4, 3)), dma((4,)), dma((4,)),
            dma((2, 4, 3)), dma((2, 4, 3)), dma((2, 4, 3)), dma((2, 4, 3)),
            dma((4,)), dma((4,)),
        ],
        compiler_params=pltpu.CompilerParams(
            collective_id=0, has_side_effects=True, vmem_limit_bytes=60 << 20
        ),
    )(sources, slowness, freq_index, coverage)


def solution(mesh):
    placed = (
        P("freq", None, "sub", None, None),
        P("sub", None, None),
        P("freq"),
        P("freq", None, None),
    )
    return jax.shard_map(
        body,
        mesh=mesh,
        in_specs=placed,
        out_specs=(P("sub", "freq", None), P("freq", "sub", None, None, None)),
        check_vma=False,
    )
```

```python
import jax
import jax.numpy as jnp
from jax import lax
from jax.experimental import pallas as pl
from jax.experimental.pallas import tpu as pltpu
from jax.sharding import PartitionSpec as P

MESH = pl.DeviceIdType.MESH
CX = 8
BAND = 16
REDUCE = ((3, 8), (2, 3), (1, 2), (0, 1))
GATHER = ((2, 8), (1, 2), (0, 1))


def smooth_plane(t):
    rows, cols = t.shape
    row = lax.broadcasted_iota(jnp.int32, t.shape, 0)
    col = lax.broadcasted_iota(jnp.int32, t.shape, 1)
    before = jnp.where(row == 0, 0.0, pltpu.roll(t, 1, 0))
    after = jnp.where(row == rows - 1, 0.0, pltpu.roll(t, rows - 1, 0))
    t = before + after + (t + t)
    before = jnp.where(col == 0, 0.0, pltpu.roll(t, 1, 1))
    after = jnp.where(col == cols - 1, 0.0, pltpu.roll(t, cols - 1, 1))
    return before + after + (t + t)


def kernel(
    src_hbm, slow_hbm, freq_ref, cover_ref, pre_ref, deliv_ref,
    src, slow, coef, v, halo, slow_x, coef_x, corr, gi, rsr, ag,
    load_sem, slow_sem, halo_ssem, halo_rsem, sx_ssem, sx_rsem, core_ssem, core_rsem,
    rs_ssem, rs_rsem, z_ssem, z_rsem, p1_ssem, p1_rsem, p2_ssem, p2_rsem, cc_ssem, cc_rsem,
):
    f = lax.axis_index("freq")
    s = lax.axis_index("sub")
    c = lax.rem(s, 2)
    zh = lax.rem(s // 2, 2)
    y = lax.rem(s // 4, 4)
    x = s // 16

    def dev(x_, y_, z_, c_):
        return {"freq": f, "sub": ((x_ * 4 + y_) * 2 + z_) * 2 + c_}

    def layer(m):
        return m + c * (CX - 1 - 2 * m)

    x_dev = {"freq": f, "sub": lax.rem(s + 2 * c + 63, 64)}
    c_dev = dev(x, y, zh, 1 - c)
    z_dev = dev(x, y, 1 - zh, c)
    xs = [dev(lax.rem(x + k, 4), y, zh, c) for k in (1, 2, 3)]
    ys = [dev(x, lax.rem(y + k, 4), zh, c) for k in (1, 2, 3)]
    fs = [{"freq": lax.rem(f + k, 4), "sub": s} for k in (1, 2, 3)]
    has_x = jnp.where((s == 0) | (s == 63), 0.0, 1.0).astype(jnp.float32)
    quarter_x = has_x * (0.25 / 16.0)

    slow_loads = [
        pltpu.make_async_copy(slow_hbm.at[layer(m)], slow.at[m], slow_sem.at[m]) for m in range(CX)
    ]
    loads = [
        pltpu.make_async_copy(src_hbm.at[:, :, layer(m)], src.at[m], load_sem.at[m]) for m in range(CX)
    ]
    for m in (0, 1, 2, 7, 3, 4, 5, 6):
        slow_loads[m].start()
        loads[m].start()

    barrier = pltpu.get_barrier_semaphore()
    partners = [x_dev, c_dev, z_dev] + xs + ys + fs
    for who in partners:
        pl.semaphore_signal(barrier, inc=1, device_id=who, device_id_type=MESH)

    weights = [1.0 + freq_ref[g].astype(jnp.float32) / 16.0 for g in range(2)]

    def remote(src_ref, dst_ref, ssem, rsem, who):
        return pltpu.make_async_remote_copy(
            src_ref=src_ref, dst_ref=dst_ref, send_sem=ssem, recv_sem=rsem,
            device_id=who, device_id_type=MESH,
        )

    def coefs(sigma):
        real = 0.875 - sigma
        inv = 1.0 / (real * real + sigma * sigma)
        return real * inv, sigma * inv

    def over_fields(step):
        def one(i, carry):
            step(i // 2, lax.rem(i, 2) * 2)
            return carry
        lax.fori_loop(0, 4, one, 0)

    def put(ref, where, g, q, h, cr, ci, add=False):
        real = h[0] * cr + h[1] * ci
        imag = h[1] * cr - h[0] * ci
        if add:
            real = real + ref[where + (g, q)]
            imag = imag + ref[where + (g, q + 1)]
        ref[where + (g, q)] = real
        ref[where + (g, q + 1)] = imag

    def first(m):
        for g in range(2):
            cr, ci = coefs((0.12 * weights[g]) * slow[m])
            coef[m, g, 0] = cr
            coef[m, g, 1] = ci
            for q in (0, 2):
                put(v, (0, m + 1), g, q, (src[m, g, q], src[m, g, q + 1]), cr, ci)

    def relax(level, m):
        def step(g, q):
            h = []
            for part in (0, 1):
                mid = v[level, m + 1, g, q + part]
                t = v[level, m, g, q + part] + v[level, m + 2, g, q + part] + (mid + mid)
                h.append(src[m, g, q + part] + (smooth_plane(t) * (1.0 / 64.0) - 0.125 * mid))
            put(v, (level + 1, m + 1), g, q, h, coef[m, g, 0], coef[m, g, 1])
        over_fields(step)

    def relax_range(level, lo, hi):
        def one(m, carry):
            relax(level, m)
            return carry
        lax.fori_loop(lo, hi, one, 0)

    def first_range(lo, hi):
        def one(m, carry):
            first(m)
            return carry
        lax.fori_loop(lo, hi, one, 0)

    for level in range(3):
        def clear(i, carry):
            v[level, 0, i // 4, lax.rem(i, 4)] = jnp.zeros((64, 256), jnp.float32)
            return carry
        lax.fori_loop(0, 8, clear, 0)

    x_sends = [
        [remote(v.at[n, 1, g], halo.at[n, g], halo_ssem.at[n, g], halo_rsem.at[n, g], x_dev) for g in range(2)]
        for n in range(3)
    ]
    quarter_rows = pl.ds(pl.multiple_of(f * BAND, BAND), BAND)
    slow_send = remote(slow.at[0, quarter_rows], slow_x.at[quarter_rows], sx_ssem.at[0], sx_rsem.at[0], x_dev)
    slow_shares = [
        remote(slow_x.at[quarter_rows], slow_x.at[quarter_rows], sx_ssem.at[1 + k], sx_rsem.at[1 + k], fs[k])
        for k in range(3)
    ]
    c_sends = [
        remote(v.at[n, 8], v.at[n, 9], core_ssem.at[n], core_rsem.at[n], c_dev) for n in range(3)
    ]

    for m in (0, 1, 2):
        slow_loads[m].wait()
        loads[m].wait()
        if m == 0:
            first(0)
            pl.semaphore_wait(barrier, len(partners))
            slow_send.start()
            x_sends[0][0].start()
            x_sends[0][1].start()
        elif m == 1:
            first(1)
            relax(0, 0)
        else:
            first(2)
            relax(0, 1)
            relax(1, 0)

    for m in (7, 3, 4, 5, 6):
        slow_loads[m].wait()
        loads[m].wait()
        if m == 7:
            first_range(7, 8)
            c_sends[0].start()
    first_range(3, 7)
    for level in range(3):
        c_sends[level].wait_recv()
        relax_range(level, 7, 8)
        if level < 2:
            c_sends[level + 1].start()
        relax_range(level, 3 if level == 2 else 2 - level, 7)

    def finish(lo, hi):
        def one(m, carry):
            for b in range(4):
                rows = pl.ds(b * BAND, BAND)
                grad = None
                for g in range(2):
                    ur, ui, ar, ai = [v[3, m + 1, g, q, rows, :] for q in range(4)]
                    gg = weights[g] * (ur * ar - ui * ai)
                    ii = weights[g] * (ur * ur + ui * ui)
                    grad, illum = (gg, ii) if grad is None else (grad + gg, illum + ii)
                gi[b, m, 0] = grad
                gi[b, m, 1] = illum
            return carry
        lax.fori_loop(lo, hi, one, 0)

    sent = []

    def rs_copies(r):
        lo, hi = REDUCE[r]
        n = pl.ds(lo, hi - lo)
        return [
            remote(gi.at[lax.rem(f + k + 1, 4), n], rsr.at[k, n],
                   rs_ssem.at[r, k], rs_rsem.at[r, k], fs[k])
            for k in range(3)
        ]

    def block(r, *where):
        lo, hi = GATHER[r]
        return ag.at[where + (pl.ds(lo, hi - lo),)]

    def z_copy(r):
        b = block(r, x, y, zh, c)
        return remote(b, b, z_ssem.at[r], z_rsem.at[r], z_dev)

    def p1_copies(r, flow):
        b = block(r, x, y, zh, c) if flow == 0 else block(r, x, y, 1 - zh, c)
        to = xs if flow == 0 else ys
        return [remote(b, b, p1_ssem.at[flow, r, k], p1_rsem.at[flow, r, k], to[k]) for k in range(3)]

    every = slice(None)

    def p2_copies(r, flow):
        b = block(r, every, y, zh, c) if flow == 0 else block(r, x, every, 1 - zh, c)
        to = ys if flow == 0 else xs
        return [remote(b, b, p2_ssem.at[flow, r, k], p2_rsem.at[flow, r, k], to[k]) for k in range(3)]

    def cc_copies(r, flow):
        out = []
        for k in range(4):
            if flow == 0:
                b = block(r, every, lax.rem(y + 4 - k, 4), zh, c)
            else:
                b = block(r, lax.rem(x + 4 - k, 4), every, 1 - zh, c)
            out.append(remote(b, b, cc_ssem.at[flow, r, k], cc_rsem.at[flow, r, k], c_dev))
        return out

    def start(copies):
        for copy in copies:
            copy.start()
            sent.append(copy)

    def arrived(copies):
        for copy in copies:
            copy.wait_recv()

    def reduce_start(r):
        finish(*REDUCE[r])
        start(rs_copies(r))

    def gather_start(r):
        for i in (0, 1) if r == 0 else (r + 1,):
            arrived(rs_copies(i))
        lo, hi = GATHER[r]

        def one(m, carry):
            grad = gi[f, m, 0] + rsr[0, m, 0] + rsr[1, m, 0] + rsr[2, m, 0]
            illum = gi[f, m, 1] + rsr[0, m, 1] + rsr[1, m, 1] + rsr[2, m, 1]
            pre = grad / jnp.sqrt(illum + 1.0)
            ag[x, y, zh, c, m] = pre
            pre_ref[layer(m)] = pre
            return carry
        lax.fori_loop(lo, hi, one, 0)
        start([z_copy(r)])
        start(p1_copies(r, 0))

    def gather_middle(r):
        arrived([z_copy(r)])
        start(p1_copies(r, 1))
        arrived(p1_copies(r, 0))
        start(p2_copies(r, 0))
        start(cc_copies(r, 0)[:1])
        arrived(p1_copies(r, 1))
        start(p2_copies(r, 1))
        start(cc_copies(r, 1)[:1])

    def gather_end(r):
        for flow in (0, 1):
            lines = p2_copies(r, flow)
            onward = cc_copies(r, flow)
            for k in (0, 2, 1):
                arrived([lines[k]])
                start([onward[k + 1]])

    C2, C3A, C3B, D2, D3 = range(5)

    def correct(ref, where, cf, terms, minus=None, add=False):
        def step(g, q):
            h = []
            for part in (0, 1):
                t = None
                for scale, tref, twhere in terms:
                    one = scale * tref[twhere + (g, q + part)]
                    t = one if t is None else t + one
                k = smooth_plane(t)
                if minus is not None:
                    k = k - 0.125 * minus[0][minus[1] + (g, q + part)]
                h.append(k)
            put(ref, where, g, q, h, cf[g, 0], cf[g, 1], add)
        over_fields(step)

    half = 0.5 / 16.0
    quarter = 0.25 / 16.0

    reduce_start(0)
    relax_range(2, 0, 3)
    x_sends[0][0].wait_send()
    x_sends[0][1].wait_send()
    x_sends[1][0].start()
    arrived(x_sends[0])
    correct(corr, (C2,), coef.at[0], [(quarter_x, halo, (0,))])
    correct(corr, (C3B,), coef.at[1], [(quarter, corr, (C2,))])
    correct(v, (3, 3), coef.at[2], [(quarter, corr, (C3B,))], add=True)
    reduce_start(1)
    slow_send.wait_recv()
    start(slow_shares)
    gather_start(0)
    x_sends[1][1].start()
    gather_middle(0)
    arrived(slow_shares)
    for g in range(2):
        cr, ci = coefs((0.12 * weights[g]) * slow_x[...])
        coef_x[g, 0] = cr
        coef_x[g, 1] = ci
    correct(corr, (D2,), coef_x, [(quarter, v, (0, 1))])
    correct(corr, (D3,), coef_x, [(half, corr, (D2,)), (quarter, v, (1, 1)), (quarter, corr, (C2,))],
            minus=(corr, (D2,)))
    x_sends[1][0].wait_send()
    x_sends[1][1].wait_send()
    x_sends[2][0].start()
    arrived(x_sends[1])
    correct(corr, (C3A,), coef.at[0],
            [(half, corr, (C2,)), (quarter_x, halo, (1,)), (quarter_x, corr, (D2,))],
            minus=(corr, (C2,)))
    correct(v, (3, 2), coef.at[1], [(half, corr, (C3B,)), (quarter, corr, (C3A,))],
            minus=(corr, (C3B,)), add=True)
    reduce_start(2)
    x_sends[2][1].start()
    correct(v, (3, 1), coef.at[0],
            [(half, corr, (C3A,)), (quarter, corr, (C3B,)), (quarter_x, corr, (D3,))],
            minus=(corr, (C3A,)), add=True)
    gather_end(0)

    arrived(x_sends[2])
    correct(v, (3, 1), coef.at[0], [(quarter_x, halo, (2,))], add=True)
    reduce_start(3)
    gather_start(1)
    gather_start(2)
    gather_middle(1)
    gather_middle(2)
    gather_end(1)
    gather_end(2)
    for r in range(len(GATHER)):
        for flow in (0, 1):
            arrived(cc_copies(r, flow))

    def pick(k, carry):
        tile = cover_ref[0, s, k]
        o = lax.shift_right_logical(tile, 3)
        j = tile & 7
        oc = o & 1
        m = j + oc * (CX - 1 - 2 * j)
        deliv_ref[0, 0, k] = ag[
            lax.shift_right_logical(o, 4), lax.shift_right_logical(o, 2) & 3,
            lax.shift_right_logical(o, 1) & 1, oc, m,
        ]
        return carry
    lax.fori_loop(0, deliv_ref.shape[2], pick, 0, unroll=8)

    for copy in x_sends[2] + [slow_send] + c_sends + sent:
        copy.wait_send()


def body(sources, slowness, freq_index, coverage):
    groups, parts, cx, nz, ny = sources.shape
    f32 = jnp.float32
    tiles = coverage.shape[2]
    vm = pltpu.VMEM
    dma = pltpu.SemaphoreType.DMA
    field = (groups, parts, nz, ny)
    return pl.pallas_call(
        kernel,
        name="inversion_step",
        out_shape=(
            jax.ShapeDtypeStruct((cx, BAND, ny), f32),
            jax.ShapeDtypeStruct((1, 1, tiles, BAND, ny), f32),
        ),
        in_specs=[
            pl.BlockSpec(memory_space=pl.ANY),
            pl.BlockSpec(memory_space=pl.ANY),
            pl.BlockSpec(memory_space=pltpu.SMEM),
            pl.BlockSpec(memory_space=pltpu.SMEM),
        ],
        out_specs=(pl.BlockSpec(memory_space=pltpu.VMEM), pl.BlockSpec(memory_space=pltpu.VMEM)),
        scratch_shapes=[
            vm((cx,) + field, f32),
            vm((cx, nz, ny), f32),
            vm((cx, groups, 2, nz, ny), f32),
            vm((4, cx + 2) + field, f32),
            vm((3,) + field, f32),
            vm((nz, ny), f32),
            vm((groups, 2, nz, ny), f32),
            vm((5,) + field, f32),
            vm((4, cx, 2, BAND, ny), f32),
            vm((3, cx, 2, BAND, ny), f32),
            vm((4, 4, 2, 2, cx, BAND, ny), f32),
            dma((cx,)), dma((cx,)),
            dma((3, 2)), dma((3, 2)), dma((4,)), dma((4,)), dma((3,)), dma((3,)),
            dma((4, 3)), dma((4, 3)), dma((4,)), dma((4,)),
            dma((2, 4, 3)), dma((2, 4, 3)), dma((2, 4, 3)), dma((2, 4, 3)),
            dma((2, 4, 4)), dma((2, 4, 4)),
        ],
        compiler_params=pltpu.CompilerParams(
            collective_id=0, has_side_effects=True, vmem_limit_bytes=60 << 20
        ),
    )(sources, slowness, freq_index, coverage)


def solution(mesh):
    placed = (
        P("freq", None, "sub", None, None),
        P("sub", None, None),
        P("freq"),
        P("freq", None, None),
    )
    return jax.shard_map(
        body,
        mesh=mesh,
        in_specs=placed,
        out_specs=(P("sub", "freq", None), P("freq", "sub", None, None, None)),
        check_vma=False,
    )
```

```python
import jax
import jax.numpy as jnp
from jax import lax
from jax.experimental import pallas as pl
from jax.experimental.pallas import tpu as pltpu
from jax.sharding import PartitionSpec as P

MESH = pl.DeviceIdType.MESH
CX = 8
BAND = 16
REDUCE = ((3, 8), (2, 3), (1, 2), (0, 1))
GATHER = ((2, 8), (1, 2), (0, 1))


def smooth_plane(t):
    rows, cols = t.shape
    row = lax.broadcasted_iota(jnp.int32, t.shape, 0)
    col = lax.broadcasted_iota(jnp.int32, t.shape, 1)
    before = jnp.where(row == 0, 0.0, pltpu.roll(t, 1, 0))
    after = jnp.where(row == rows - 1, 0.0, pltpu.roll(t, rows - 1, 0))
    t = before + after + (t + t)
    before = jnp.where(col == 0, 0.0, pltpu.roll(t, 1, 1))
    after = jnp.where(col == cols - 1, 0.0, pltpu.roll(t, cols - 1, 1))
    return before + after + (t + t)


def kernel(
    src_hbm, slow_hbm, freq_ref, cover_ref, pre_ref, deliv_ref,
    src, slow, coef, v, halo, slow_x, coef_x, corr, gi, rsr, near, far, ag,
    load_sem, slow_sem, halo_ssem, halo_rsem, sx_ssem, sx_rsem, core_ssem, core_rsem,
    rs_ssem, rs_rsem, z_ssem, z_rsem, p1_ssem, p1_rsem, p2_ssem, p2_rsem, cc_ssem, cc_rsem,
):
    f = lax.axis_index("freq")
    s = lax.axis_index("sub")
    c = lax.rem(s, 2)
    zh = lax.rem(s // 2, 2)
    y = lax.rem(s // 4, 4)
    x = s // 16

    def dev(x_, y_, z_, c_):
        return {"freq": f, "sub": ((x_ * 4 + y_) * 2 + z_) * 2 + c_}

    def layer(m):
        return m + c * (CX - 1 - 2 * m)

    x_dev = {"freq": f, "sub": lax.rem(s + 2 * c + 63, 64)}
    c_dev = dev(x, y, zh, 1 - c)
    z_dev = dev(x, y, 1 - zh, c)
    xs = [dev(lax.rem(x + k, 4), y, zh, c) for k in (1, 2, 3)]
    ys = [dev(x, lax.rem(y + k, 4), zh, c) for k in (1, 2, 3)]
    fs = [{"freq": lax.rem(f + k, 4), "sub": s} for k in (1, 2, 3)]
    near_dev = {"freq": f + 1 - 2 * lax.rem(f, 2), "sub": s}
    far_dev = fs[1]
    has_x = jnp.where((s == 0) | (s == 63), 0.0, 1.0).astype(jnp.float32)
    quarter_x = has_x * (0.25 / 16.0)

    slow_loads = [
        pltpu.make_async_copy(slow_hbm.at[layer(m)], slow.at[m], slow_sem.at[m]) for m in range(CX)
    ]
    loads = [
        pltpu.make_async_copy(src_hbm.at[:, :, layer(m)], src.at[m], load_sem.at[m]) for m in range(CX)
    ]
    for m in (0, 1, 2, 7, 3, 4, 5, 6):
        slow_loads[m].start()
        loads[m].start()

    barrier = pltpu.get_barrier_semaphore()
    partners = [x_dev, c_dev, z_dev] + xs + ys + fs
    for who in partners:
        pl.semaphore_signal(barrier, inc=1, device_id=who, device_id_type=MESH)

    weights = [1.0 + freq_ref[g].astype(jnp.float32) / 16.0 for g in range(2)]

    def remote(src_ref, dst_ref, ssem, rsem, who):
        return pltpu.make_async_remote_copy(
            src_ref=src_ref, dst_ref=dst_ref, send_sem=ssem, recv_sem=rsem,
            device_id=who, device_id_type=MESH,
        )

    def coefs(sigma):
        real = 0.875 - sigma
        inv = 1.0 / (real * real + sigma * sigma)
        return real * inv, sigma * inv

    def over_fields(step):
        def one(i, carry):
            step(i // 2, lax.rem(i, 2) * 2)
            return carry
        lax.fori_loop(0, 4, one, 0)

    def put(ref, where, g, q, h, cr, ci, add=False):
        real = h[0] * cr + h[1] * ci
        imag = h[1] * cr - h[0] * ci
        if add:
            real = real + ref[where + (g, q)]
            imag = imag + ref[where + (g, q + 1)]
        ref[where + (g, q)] = real
        ref[where + (g, q + 1)] = imag

    def first(m):
        for g in range(2):
            cr, ci = coefs((0.12 * weights[g]) * slow[m])
            coef[m, g, 0] = cr
            coef[m, g, 1] = ci
            for q in (0, 2):
                put(v, (0, m + 1), g, q, (src[m, g, q], src[m, g, q + 1]), cr, ci)

    def relax(level, m):
        def step(g, q):
            h = []
            for part in (0, 1):
                mid = v[level, m + 1, g, q + part]
                t = v[level, m, g, q + part] + v[level, m + 2, g, q + part] + (mid + mid)
                h.append(src[m, g, q + part] + (smooth_plane(t) * (1.0 / 64.0) - 0.125 * mid))
            put(v, (level + 1, m + 1), g, q, h, coef[m, g, 0], coef[m, g, 1])
        over_fields(step)

    def relax_range(level, lo, hi):
        def one(m, carry):
            relax(level, m)
            return carry
        lax.fori_loop(lo, hi, one, 0)

    def first_range(lo, hi):
        def one(m, carry):
            first(m)
            return carry
        lax.fori_loop(lo, hi, one, 0)

    for level in range(3):
        def clear(i, carry):
            v[level, 0, i // 4, lax.rem(i, 4)] = jnp.zeros((64, 256), jnp.float32)
            return carry
        lax.fori_loop(0, 8, clear, 0)

    x_sends = [
        [remote(v.at[n, 1, g], halo.at[n, g], halo_ssem.at[n, g], halo_rsem.at[n, g], x_dev) for g in range(2)]
        for n in range(3)
    ]
    quarter_rows = pl.ds(pl.multiple_of(f * BAND, BAND), BAND)
    slow_send = remote(slow.at[0, quarter_rows], slow_x.at[quarter_rows], sx_ssem.at[0], sx_rsem.at[0], x_dev)
    slow_shares = [
        remote(slow_x.at[quarter_rows], slow_x.at[quarter_rows], sx_ssem.at[1 + k], sx_rsem.at[1 + k], fs[k])
        for k in range(3)
    ]
    c_sends = [
        remote(v.at[n, 8], v.at[n, 9], core_ssem.at[n], core_rsem.at[n], c_dev) for n in range(3)
    ]

    for m in (0, 1, 2):
        slow_loads[m].wait()
        loads[m].wait()
        if m == 0:
            first(0)
            pl.semaphore_wait(barrier, len(partners))
            slow_send.start()
            x_sends[0][0].start()
            x_sends[0][1].start()
        elif m == 1:
            first(1)
            relax(0, 0)
        else:
            first(2)
            relax(0, 1)
            relax(1, 0)

    for m in (7, 3, 4, 5, 6):
        slow_loads[m].wait()
        loads[m].wait()
        if m == 7:
            first_range(7, 8)
            c_sends[0].start()
    first_range(3, 7)
    for level in range(3):
        c_sends[level].wait_recv()
        relax_range(level, 7, 8)
        if level < 2:
            c_sends[level + 1].start()
        relax_range(level, 3 if level == 2 else 2 - level, 7)

    def finish(lo, hi):
        def one(m, carry):
            for b in range(4):
                rows = pl.ds(b * BAND, BAND)
                grad = None
                for g in range(2):
                    ur, ui, ar, ai = [v[3, m + 1, g, q, rows, :] for q in range(4)]
                    gg = weights[g] * (ur * ar - ui * ai)
                    ii = weights[g] * (ur * ur + ui * ui)
                    grad, illum = (gg, ii) if grad is None else (grad + gg, illum + ii)
                gi[b // 2, b % 2, m, 0] = grad
                gi[b // 2, b % 2, m, 1] = illum
            return carry
        lax.fori_loop(lo, hi, one, 0)

    sent = []

    fj, fp = f // 2, lax.rem(f, 2)

    def rs_copies(r):
        lo, hi = REDUCE[r]
        n = pl.ds(lo, hi - lo)
        out = []
        for k in range(3):
            to = lax.rem(f + k + 1, 4)
            out.append(remote(gi.at[to // 2, lax.rem(to, 2), n], rsr.at[k, n],
                              rs_ssem.at[r, k], rs_rsem.at[r, k], fs[k]))
        return out

    def near_copy(r):
        lo, hi = REDUCE[r]
        n = pl.ds(lo, hi - lo)
        return remote(gi.at[:, 1 - fp, n], near.at[:, n], rs_ssem.at[r, 0], rs_rsem.at[r, 0], near_dev)

    def far_copy(r):
        lo, hi = REDUCE[r]
        n = pl.ds(lo, hi - lo)
        return remote(near.at[1 - fj, n], far.at[n], rs_ssem.at[r, 1], rs_rsem.at[r, 1], far_dev)

    def reduce_far(r):
        arrived([near_copy(r)])

        def one(m, carry):
            for part in range(2):
                for j in range(2):
                    near[j, m, part] = near[j, m, part] + gi[j, fp, m, part]
            return carry
        lax.fori_loop(*REDUCE[r], one, 0)
        start([far_copy(r)])

    def block(r, *where):
        lo, hi = GATHER[r]
        return ag.at[where + (pl.ds(lo, hi - lo),)]

    def z_copy(r):
        b = block(r, x, y, zh, c)
        return remote(b, b, z_ssem.at[r], z_rsem.at[r], z_dev)

    def p1_copies(r, flow):
        b = block(r, x, y, zh, c) if flow == 0 else block(r, x, y, 1 - zh, c)
        to = xs if flow == 0 else ys
        return [remote(b, b, p1_ssem.at[flow, r, k], p1_rsem.at[flow, r, k], to[k]) for k in range(3)]

    every = slice(None)

    def p2_copies(r, flow):
        b = block(r, every, y, zh, c) if flow == 0 else block(r, x, every, 1 - zh, c)
        to = ys if flow == 0 else xs
        return [remote(b, b, p2_ssem.at[flow, r, k], p2_rsem.at[flow, r, k], to[k]) for k in range(3)]

    def cc_copies(r, flow):
        out = []
        for k in range(4):
            if flow == 0:
                b = block(r, every, lax.rem(y + 4 - k, 4), zh, c)
            else:
                b = block(r, lax.rem(x + 4 - k, 4), every, 1 - zh, c)
            out.append(remote(b, b, cc_ssem.at[flow, r, k], cc_rsem.at[flow, r, k], c_dev))
        return out

    def start(copies):
        for copy in copies:
            copy.start()
            sent.append(copy)

    def arrived(copies):
        for copy in copies:
            copy.wait_recv()

    def reduce_start(r):
        finish(*REDUCE[r])
        start([near_copy(r)] if r < 2 else rs_copies(r))

    def gather_start(r):
        lo, hi = GATHER[r]
        if r == 0:
            arrived([far_copy(0)])
            arrived([far_copy(1)])
        else:
            arrived(rs_copies(r + 1))

        def one(m, carry):
            if r == 0:
                grad, illum = [near[fj, m, part] + far[m, part] for part in range(2)]
            else:
                grad, illum = [
                    gi[fj, fp, m, part] + rsr[0, m, part] + rsr[1, m, part] + rsr[2, m, part]
                    for part in range(2)
                ]
            pre = grad / jnp.sqrt(illum + 1.0)
            ag[x, y, zh, c, m] = pre
            pre_ref[layer(m)] = pre
            return carry
        lax.fori_loop(lo, hi, one, 0)
        start([z_copy(r)])
        start(p1_copies(r, 0))

    def gather_middle(r):
        arrived([z_copy(r)])
        start(p1_copies(r, 1))
        arrived(p1_copies(r, 0))
        start(p2_copies(r, 0))
        start(cc_copies(r, 0)[:1])
        arrived(p1_copies(r, 1))
        start(p2_copies(r, 1))
        start(cc_copies(r, 1)[:1])

    def gather_end(r):
        for flow in (0, 1):
            lines = p2_copies(r, flow)
            onward = cc_copies(r, flow)
            for k in (0, 2, 1):
                arrived([lines[k]])
                start([onward[k + 1]])

    C2, C3A, C3B, D2, D3 = range(5)

    def correct(ref, where, cf, terms, minus=None, add=False):
        def step(g, q):
            h = []
            for part in (0, 1):
                t = None
                for scale, tref, twhere in terms:
                    one = scale * tref[twhere + (g, q + part)]
                    t = one if t is None else t + one
                k = smooth_plane(t)
                if minus is not None:
                    k = k - 0.125 * minus[0][minus[1] + (g, q + part)]
                h.append(k)
            put(ref, where, g, q, h, cf[g, 0], cf[g, 1], add)
        over_fields(step)

    half = 0.5 / 16.0
    quarter = 0.25 / 16.0

    reduce_start(0)
    relax_range(2, 0, 3)
    x_sends[0][0].wait_send()
    x_sends[0][1].wait_send()
    arrived(x_sends[0])
    correct(corr, (C2,), coef.at[0], [(quarter_x, halo, (0,))])
    correct(corr, (C3B,), coef.at[1], [(quarter, corr, (C2,))])
    correct(v, (3, 3), coef.at[2], [(quarter, corr, (C3B,))], add=True)
    reduce_start(1)
    slow_send.wait_recv()
    start(slow_shares)
    reduce_far(0)
    reduce_far(1)
    gather_start(0)
    x_sends[1][0].start()
    x_sends[1][1].start()
    gather_middle(0)
    arrived(slow_shares)
    for g in range(2):
        cr, ci = coefs((0.12 * weights[g]) * slow_x[...])
        coef_x[g, 0] = cr
        coef_x[g, 1] = ci
    correct(corr, (D2,), coef_x, [(quarter, v, (0, 1))])
    correct(corr, (D3,), coef_x, [(half, corr, (D2,)), (quarter, v, (1, 1)), (quarter, corr, (C2,))],
            minus=(corr, (D2,)))
    x_sends[1][0].wait_send()
    x_sends[1][1].wait_send()
    x_sends[2][0].start()
    arrived(x_sends[1])
    correct(corr, (C3A,), coef.at[0],
            [(half, corr, (C2,)), (quarter_x, halo, (1,)), (quarter_x, corr, (D2,))],
            minus=(corr, (C2,)))
    correct(v, (3, 2), coef.at[1], [(half, corr, (C3B,)), (quarter, corr, (C3A,))],
            minus=(corr, (C3B,)), add=True)
    reduce_start(2)
    x_sends[2][1].start()
    correct(v, (3, 1), coef.at[0],
            [(half, corr, (C3A,)), (quarter, corr, (C3B,)), (quarter_x, corr, (D3,))],
            minus=(corr, (C3A,)), add=True)
    gather_end(0)

    arrived(x_sends[2])
    correct(v, (3, 1), coef.at[0], [(quarter_x, halo, (2,))], add=True)
    reduce_start(3)
    gather_start(1)
    gather_start(2)
    gather_middle(1)
    gather_middle(2)
    gather_end(1)
    gather_end(2)
    for r in range(len(GATHER)):
        for flow in (0, 1):
            arrived(cc_copies(r, flow))

    def pick(k, carry):
        tile = cover_ref[0, s, k]
        o = lax.shift_right_logical(tile, 3)
        j = tile & 7
        oc = o & 1
        m = j + oc * (CX - 1 - 2 * j)
        deliv_ref[0, 0, k] = ag[
            lax.shift_right_logical(o, 4), lax.shift_right_logical(o, 2) & 3,
            lax.shift_right_logical(o, 1) & 1, oc, m,
        ]
        return carry
    lax.fori_loop(0, deliv_ref.shape[2], pick, 0, unroll=8)

    for copy in x_sends[2] + [slow_send] + c_sends + sent:
        copy.wait_send()


def body(sources, slowness, freq_index, coverage):
    groups, parts, cx, nz, ny = sources.shape
    f32 = jnp.float32
    tiles = coverage.shape[2]
    vm = pltpu.VMEM
    dma = pltpu.SemaphoreType.DMA
    field = (groups, parts, nz, ny)
    return pl.pallas_call(
        kernel,
        name="inversion_step",
        out_shape=(
            vm((cx, BAND, ny), f32),
            vm((1, 1, tiles, BAND, ny), f32),
        ),
        in_specs=[
            pl.BlockSpec(memory_space=pl.ANY),
            pl.BlockSpec(memory_space=pl.ANY),
            pl.BlockSpec(memory_space=pltpu.SMEM),
            pl.BlockSpec(memory_space=pltpu.SMEM),
        ],
        out_specs=(pl.BlockSpec(memory_space=pltpu.VMEM), pl.BlockSpec(memory_space=pltpu.VMEM)),
        scratch_shapes=[
            vm((cx,) + field, f32),
            vm((cx, nz, ny), f32),
            vm((cx, groups, 2, nz, ny), f32),
            vm((4, cx + 2) + field, f32),
            vm((3,) + field, f32),
            vm((nz, ny), f32),
            vm((groups, 2, nz, ny), f32),
            vm((5,) + field, f32),
            vm((2, 2, cx, 2, BAND, ny), f32),
            vm((3, cx, 2, BAND, ny), f32),
            vm((2, cx, 2, BAND, ny), f32),
            vm((cx, 2, BAND, ny), f32),
            vm((4, 4, 2, 2, cx, BAND, ny), f32),
            dma((cx,)), dma((cx,)),
            dma((3, 2)), dma((3, 2)), dma((4,)), dma((4,)), dma((3,)), dma((3,)),
            dma((4, 3)), dma((4, 3)), dma((4,)), dma((4,)),
            dma((2, 4, 3)), dma((2, 4, 3)), dma((2, 4, 3)), dma((2, 4, 3)),
            dma((2, 4, 4)), dma((2, 4, 4)),
        ],
        compiler_params=pltpu.CompilerParams(
            collective_id=0, has_side_effects=True, vmem_limit_bytes=60 << 20
        ),
    )(sources, slowness, freq_index, coverage)


def solution(mesh):
    placed = (
        P("freq", None, "sub", None, None),
        P("sub", None, None),
        P("freq"),
        P("freq", None, None),
    )
    return jax.shard_map(
        body,
        mesh=mesh,
        in_specs=placed,
        out_specs=(P("sub", "freq", None), P("freq", "sub", None, None, None)),
        check_vma=False,
    )
```

```python
import jax
import jax.numpy as jnp
from jax import lax
from jax.experimental import pallas as pl
from jax.experimental.pallas import tpu as pltpu
from jax.sharding import PartitionSpec as P

MESH = pl.DeviceIdType.MESH
CX = 8
BAND = 16
REDUCE = ((3, 8), (2, 3), (1, 2), (0, 1))
GATHER = ((2, 8), (1, 2), (0, 1))


def smooth_plane(t):
    rows, cols = t.shape
    row = lax.broadcasted_iota(jnp.int32, t.shape, 0)
    col = lax.broadcasted_iota(jnp.int32, t.shape, 1)
    before = jnp.where(row == 0, 0.0, pltpu.roll(t, 1, 0))
    after = jnp.where(row == rows - 1, 0.0, pltpu.roll(t, rows - 1, 0))
    t = before + after + (t + t)
    before = jnp.where(col == 0, 0.0, pltpu.roll(t, 1, 1))
    after = jnp.where(col == cols - 1, 0.0, pltpu.roll(t, cols - 1, 1))
    return before + after + (t + t)


def kernel(
    src_hbm, slow_hbm, freq_ref, cover_ref, pre_ref, deliv_ref,
    src, slow, coef, v, halo, slow_x, coef_x, corr, gi, rsr, near, far, ag,
    load_sem, slow_sem, halo_ssem, halo_rsem, sx_ssem, sx_rsem, core_ssem, core_rsem,
    rs_ssem, rs_rsem, z_ssem, z_rsem, p1_ssem, p1_rsem, p2_ssem, p2_rsem, cc_ssem, cc_rsem,
):
    f = lax.axis_index("freq")
    s = lax.axis_index("sub")
    c = lax.rem(s, 2)
    zh = lax.rem(s // 2, 2)
    y = lax.rem(s // 4, 4)
    x = s // 16

    def dev(x_, y_, z_, c_):
        return {"freq": f, "sub": ((x_ * 4 + y_) * 2 + z_) * 2 + c_}

    def layer(m):
        return m + c * (CX - 1 - 2 * m)

    x_dev = {"freq": f, "sub": lax.rem(s + 2 * c + 63, 64)}
    c_dev = dev(x, y, zh, 1 - c)
    z_dev = dev(x, y, 1 - zh, c)
    xs = [dev(lax.rem(x + k, 4), y, zh, c) for k in (1, 2, 3)]
    ys = [dev(x, lax.rem(y + k, 4), zh, c) for k in (1, 2, 3)]
    fs = [{"freq": lax.rem(f + k, 4), "sub": s} for k in (1, 2, 3)]
    near_dev = {"freq": f + 1 - 2 * lax.rem(f, 2), "sub": s}
    far_dev = fs[1]
    has_x = jnp.where((s == 0) | (s == 63), 0.0, 1.0).astype(jnp.float32)
    quarter_x = has_x * (0.25 / 16.0)

    slow_loads = [
        pltpu.make_async_copy(slow_hbm.at[layer(m)], slow.at[m], slow_sem.at[m]) for m in range(CX)
    ]
    loads = [
        pltpu.make_async_copy(src_hbm.at[:, :, layer(m)], src.at[m], load_sem.at[m]) for m in range(CX)
    ]
    for m in (0, 1, 2, 7, 3, 4, 5, 6):
        slow_loads[m].start()
        loads[m].start()

    barrier = pltpu.get_barrier_semaphore()
    partners = [x_dev, c_dev, z_dev] + xs + ys + fs
    for who in partners:
        pl.semaphore_signal(barrier, inc=1, device_id=who, device_id_type=MESH)

    weights = [1.0 + freq_ref[g].astype(jnp.float32) / 16.0 for g in range(2)]

    def remote(src_ref, dst_ref, ssem, rsem, who):
        return pltpu.make_async_remote_copy(
            src_ref=src_ref, dst_ref=dst_ref, send_sem=ssem, recv_sem=rsem,
            device_id=who, device_id_type=MESH,
        )

    def coefs(sigma):
        real = 0.875 - sigma
        inv = 1.0 / (real * real + sigma * sigma)
        return real * inv, sigma * inv

    def over_fields(step):
        def one(i, carry):
            step(i // 2, lax.rem(i, 2) * 2)
            return carry
        lax.fori_loop(0, 4, one, 0)

    def put(ref, where, g, q, h, cr, ci, add=False):
        real = h[0] * cr + h[1] * ci
        imag = h[1] * cr - h[0] * ci
        if add:
            real = real + ref[where + (g, q)]
            imag = imag + ref[where + (g, q + 1)]
        ref[where + (g, q)] = real
        ref[where + (g, q + 1)] = imag

    def first(m):
        for g in range(2):
            cr, ci = coefs((0.12 * weights[g]) * slow[m])
            coef[m, g, 0] = cr
            coef[m, g, 1] = ci
            for q in (0, 2):
                put(v, (0, m + 1), g, q, (src[m, g, q], src[m, g, q + 1]), cr, ci)

    def relax(level, m):
        def step(g, q):
            h = []
            for part in (0, 1):
                mid = v[level, m + 1, g, q + part]
                t = v[level, m, g, q + part] + v[level, m + 2, g, q + part] + (mid + mid)
                h.append(src[m, g, q + part] + (smooth_plane(t) * (1.0 / 64.0) - 0.125 * mid))
            put(v, (level + 1, m + 1), g, q, h, coef[m, g, 0], coef[m, g, 1])
        over_fields(step)

    def relax_range(level, lo, hi):
        def one(m, carry):
            relax(level, m)
            return carry
        lax.fori_loop(lo, hi, one, 0)

    def first_range(lo, hi):
        def one(m, carry):
            first(m)
            return carry
        lax.fori_loop(lo, hi, one, 0)

    for level in range(3):
        def clear(i, carry):
            v[level, 0, i // 4, lax.rem(i, 4)] = jnp.zeros((64, 256), jnp.float32)
            return carry
        lax.fori_loop(0, 8, clear, 0)

    x_sends = [
        [remote(v.at[n, 1, g], halo.at[n, g], halo_ssem.at[n, g], halo_rsem.at[n, g], x_dev) for g in range(2)]
        for n in range(3)
    ]
    quarter_rows = pl.ds(pl.multiple_of(f * BAND, BAND), BAND)
    slow_send = remote(slow.at[0, quarter_rows], slow_x.at[quarter_rows], sx_ssem.at[0], sx_rsem.at[0], x_dev)
    slow_shares = [
        remote(slow_x.at[quarter_rows], slow_x.at[quarter_rows], sx_ssem.at[1 + k], sx_rsem.at[1 + k], fs[k])
        for k in range(3)
    ]
    c_sends = [
        remote(v.at[n, 8], v.at[n, 9], core_ssem.at[n], core_rsem.at[n], c_dev) for n in range(3)
    ]

    for m in (0, 1, 2):
        slow_loads[m].wait()
        loads[m].wait()
        if m == 0:
            first(0)
            pl.semaphore_wait(barrier, len(partners))
            slow_send.start()
            x_sends[0][0].start()
            x_sends[0][1].start()
        elif m == 1:
            first(1)
            relax(0, 0)
        else:
            first(2)
            relax(0, 1)
            relax(1, 0)

    for m in (7, 3, 4, 5, 6):
        slow_loads[m].wait()
        loads[m].wait()
        if m == 7:
            first_range(7, 8)
            c_sends[0].start()
    first_range(3, 7)
    for level in range(3):
        c_sends[level].wait_recv()
        relax_range(level, 7, 8)
        if level < 2:
            c_sends[level + 1].start()
        relax_range(level, 3 if level == 2 else 2 - level, 7)

    def finish(lo, hi):
        def one(m, carry):
            for b in range(4):
                rows = pl.ds(b * BAND, BAND)
                grad = None
                for g in range(2):
                    ur, ui, ar, ai = [v[3, m + 1, g, q, rows, :] for q in range(4)]
                    gg = weights[g] * (ur * ar - ui * ai)
                    ii = weights[g] * (ur * ur + ui * ui)
                    grad, illum = (gg, ii) if grad is None else (grad + gg, illum + ii)
                gi[b // 2, b % 2, m, 0] = grad
                gi[b // 2, b % 2, m, 1] = illum
            return carry
        lax.fori_loop(lo, hi, one, 0)

    sent = []

    fj, fp = f // 2, lax.rem(f, 2)

    def rs_copies(r):
        lo, hi = REDUCE[r]
        n = pl.ds(lo, hi - lo)
        out = []
        for k in range(3):
            to = lax.rem(f + k + 1, 4)
            out.append(remote(gi.at[to // 2, lax.rem(to, 2), n], rsr.at[k, n],
                              rs_ssem.at[r, k], rs_rsem.at[r, k], fs[k]))
        return out

    def near_copy(r):
        lo, hi = REDUCE[r]
        n = pl.ds(lo, hi - lo)
        return remote(gi.at[:, 1 - fp, n], near.at[:, n], rs_ssem.at[r, 0], rs_rsem.at[r, 0], near_dev)

    def far_copy(r):
        lo, hi = REDUCE[r]
        n = pl.ds(lo, hi - lo)
        return remote(near.at[1 - fj, n], far.at[n], rs_ssem.at[r, 1], rs_rsem.at[r, 1], far_dev)

    def reduce_far(r):
        arrived([near_copy(r)])

        def one(m, carry):
            for part in range(2):
                for j in range(2):
                    near[j, m, part] = near[j, m, part] + gi[j, fp, m, part]
            return carry
        lax.fori_loop(*REDUCE[r], one, 0)
        start([far_copy(r)])

    def block(r, *where):
        lo, hi = GATHER[r]
        return ag.at[where + (pl.ds(lo, hi - lo),)]

    def z_copy(r):
        b = block(r, x, y, zh, c)
        return remote(b, b, z_ssem.at[r], z_rsem.at[r], z_dev)

    def p1_copies(r, flow):
        b = block(r, x, y, zh, c) if flow == 0 else block(r, x, y, 1 - zh, c)
        to = xs if flow == 0 else ys
        return [remote(b, b, p1_ssem.at[flow, r, k], p1_rsem.at[flow, r, k], to[k]) for k in range(3)]

    every = slice(None)

    def p2_copies(r, flow):
        b = block(r, every, y, zh, c) if flow == 0 else block(r, x, every, 1 - zh, c)
        to = ys if flow == 0 else xs
        return [remote(b, b, p2_ssem.at[flow, r, k], p2_rsem.at[flow, r, k], to[k]) for k in range(3)]

    def cc_copies(r, flow):
        out = []
        for k in range(4):
            if flow == 0:
                b = block(r, every, lax.rem(y + 4 - k, 4), zh, c)
            else:
                b = block(r, lax.rem(x + 4 - k, 4), every, 1 - zh, c)
            out.append(remote(b, b, cc_ssem.at[flow, r, k], cc_rsem.at[flow, r, k], c_dev))
        return out

    def start(copies):
        for copy in copies:
            copy.start()
            sent.append(copy)

    def arrived(copies):
        for copy in copies:
            copy.wait_recv()

    def reduce_start(r):
        finish(*REDUCE[r])
        start([near_copy(r)] if r < 1 else rs_copies(r))

    def gather_start(r):
        lo, hi = GATHER[r]
        if r == 0:
            arrived([far_copy(0)])
            arrived(rs_copies(1))
        else:
            arrived(rs_copies(r + 1))

        def one(m, carry, summed=(r == 0)):
            if summed:
                grad, illum = [near[fj, m, part] + far[m, part] for part in range(2)]
            else:
                grad, illum = [
                    gi[fj, fp, m, part] + rsr[0, m, part] + rsr[1, m, part] + rsr[2, m, part]
                    for part in range(2)
                ]
            pre = grad / jnp.sqrt(illum + 1.0)
            ag[x, y, zh, c, m] = pre
            pre_ref[layer(m)] = pre
            return carry
        if r == 0:
            one(2, 0, False)
            lo = 3
        lax.fori_loop(lo, hi, one, 0)
        start([z_copy(r)])
        start(p1_copies(r, 0))

    def gather_middle(r):
        arrived([z_copy(r)])
        start(p1_copies(r, 1))
        arrived(p1_copies(r, 0))
        start(p2_copies(r, 0))
        start(cc_copies(r, 0)[:1])
        arrived(p1_copies(r, 1))
        start(p2_copies(r, 1))
        start(cc_copies(r, 1)[:1])

    def gather_end(r):
        for flow in (0, 1):
            lines = p2_copies(r, flow)
            onward = cc_copies(r, flow)
            for k in (0, 2, 1):
                arrived([lines[k]])
                start([onward[k + 1]])

    C2, C3A, C3B, D2, D3 = range(5)

    def correct(ref, where, cf, terms, minus=None, add=False):
        def step(g, q):
            h = []
            for part in (0, 1):
                t = None
                for scale, tref, twhere in terms:
                    one = scale * tref[twhere + (g, q + part)]
                    t = one if t is None else t + one
                k = smooth_plane(t)
                if minus is not None:
                    k = k - 0.125 * minus[0][minus[1] + (g, q + part)]
                h.append(k)
            put(ref, where, g, q, h, cf[g, 0], cf[g, 1], add)
        over_fields(step)

    half = 0.5 / 16.0
    quarter = 0.25 / 16.0

    reduce_start(0)
    relax_range(2, 0, 3)
    x_sends[0][0].wait_send()
    x_sends[0][1].wait_send()
    arrived(x_sends[0])
    correct(corr, (C2,), coef.at[0], [(quarter_x, halo, (0,))])
    correct(corr, (C3B,), coef.at[1], [(quarter, corr, (C2,))])
    correct(v, (3, 3), coef.at[2], [(quarter, corr, (C3B,))], add=True)
    reduce_start(1)
    slow_send.wait_recv()
    start(slow_shares)
    reduce_far(0)
    gather_start(0)
    x_sends[1][0].start()
    x_sends[1][1].start()
    gather_middle(0)
    arrived(slow_shares)
    for g in range(2):
        cr, ci = coefs((0.12 * weights[g]) * slow_x[...])
        coef_x[g, 0] = cr
        coef_x[g, 1] = ci
    correct(corr, (D2,), coef_x, [(quarter, v, (0, 1))])
    correct(corr, (D3,), coef_x, [(half, corr, (D2,)), (quarter, v, (1, 1)), (quarter, corr, (C2,))],
            minus=(corr, (D2,)))
    x_sends[1][0].wait_send()
    x_sends[1][1].wait_send()
    x_sends[2][0].start()
    arrived(x_sends[1])
    correct(corr, (C3A,), coef.at[0],
            [(half, corr, (C2,)), (quarter_x, halo, (1,)), (quarter_x, corr, (D2,))],
            minus=(corr, (C2,)))
    correct(v, (3, 2), coef.at[1], [(half, corr, (C3B,)), (quarter, corr, (C3A,))],
            minus=(corr, (C3B,)), add=True)
    reduce_start(2)
    x_sends[2][1].start()
    correct(v, (3, 1), coef.at[0],
            [(half, corr, (C3A,)), (quarter, corr, (C3B,)), (quarter_x, corr, (D3,))],
            minus=(corr, (C3A,)), add=True)
    gather_end(0)

    arrived(x_sends[2])
    correct(v, (3, 1), coef.at[0], [(quarter_x, halo, (2,))], add=True)
    reduce_start(3)
    gather_start(1)
    gather_start(2)
    gather_middle(1)
    gather_middle(2)
    gather_end(1)
    gather_end(2)
    for r in range(len(GATHER)):
        for flow in (0, 1):
            arrived(cc_copies(r, flow))

    def pick(k, carry):
        tile = cover_ref[0, s, k]
        o = lax.shift_right_logical(tile, 3)
        j = tile & 7
        oc = o & 1
        m = j + oc * (CX - 1 - 2 * j)
        deliv_ref[0, 0, k] = ag[
            lax.shift_right_logical(o, 4), lax.shift_right_logical(o, 2) & 3,
            lax.shift_right_logical(o, 1) & 1, oc, m,
        ]
        return carry
    lax.fori_loop(0, deliv_ref.shape[2], pick, 0, unroll=8)

    for copy in x_sends[2] + [slow_send] + c_sends + sent:
        copy.wait_send()


def body(sources, slowness, freq_index, coverage):
    groups, parts, cx, nz, ny = sources.shape
    f32 = jnp.float32
    tiles = coverage.shape[2]
    vm = pltpu.VMEM
    dma = pltpu.SemaphoreType.DMA
    field = (groups, parts, nz, ny)
    return pl.pallas_call(
        kernel,
        name="inversion_step",
        out_shape=(
            vm((cx, BAND, ny), f32),
            vm((1, 1, tiles, BAND, ny), f32),
        ),
        in_specs=[
            pl.BlockSpec(memory_space=pl.ANY),
            pl.BlockSpec(memory_space=pl.ANY),
            pl.BlockSpec(memory_space=pltpu.SMEM),
            pl.BlockSpec(memory_space=pltpu.SMEM),
        ],
        out_specs=(pl.BlockSpec(memory_space=pltpu.VMEM), pl.BlockSpec(memory_space=pltpu.VMEM)),
        scratch_shapes=[
            vm((cx,) + field, f32),
            vm((cx, nz, ny), f32),
            vm((cx, groups, 2, nz, ny), f32),
            vm((4, cx + 2) + field, f32),
            vm((3,) + field, f32),
            vm((nz, ny), f32),
            vm((groups, 2, nz, ny), f32),
            vm((5,) + field, f32),
            vm((2, 2, cx, 2, BAND, ny), f32),
            vm((3, cx, 2, BAND, ny), f32),
            vm((2, cx, 2, BAND, ny), f32),
            vm((cx, 2, BAND, ny), f32),
            vm((4, 4, 2, 2, cx, BAND, ny), f32),
            dma((cx,)), dma((cx,)),
            dma((3, 2)), dma((3, 2)), dma((4,)), dma((4,)), dma((3,)), dma((3,)),
            dma((4, 3)), dma((4, 3)), dma((4,)), dma((4,)),
            dma((2, 4, 3)), dma((2, 4, 3)), dma((2, 4, 3)), dma((2, 4, 3)),
            dma((2, 4, 4)), dma((2, 4, 4)),
        ],
        compiler_params=pltpu.CompilerParams(
            collective_id=0, has_side_effects=True, vmem_limit_bytes=60 << 20
        ),
    )(sources, slowness, freq_index, coverage)


def solution(mesh):
    placed = (
        P("freq", None, "sub", None, None),
        P("sub", None, None),
        P("freq"),
        P("freq", None, None),
    )
    return jax.shard_map(
        body,
        mesh=mesh,
        in_specs=placed,
        out_specs=(P("sub", "freq", None), P("freq", "sub", None, None, None)),
        check_vma=False,
    )
```
